768 devices in a mesh: section: 8 (over y_lo, core), dp: 96 (over y_hi, x, z).
Axes of the slice: x: 4, y: 8 (y_hi: 2, y_lo: 4; y = y_hi * 4 + y_lo), z: 12, core: 2. Of those that a mesh axis runs over, the one named last changes fastest.
Arguments:
- queries: bfloat16 [8, 12288, 8192], P('section', 'dp'), may hold values from -48 to 48
- image_kv: bfloat16 [8, 2, 768, 1024], P(None, None, ('section', 'dp')), may hold values from -4 to 4
- visible: int32 [12288], P('dp'), may hold values from 0 to 768, as said below
- gate: float32 [8], P('section'), may hold values from 0.3 to 2
Outputs:
- cross_out: bfloat16 [8, 12288, 8192], P('section', 'dp')
The draws below stay inside these ranges and needn't reach their ends.
Inputs may be any that keep to these rules, and one draw needn't show every extreme that they name: `visible`: every value is a multiple of 192; the last token of each aligned block of 128 text tokens sees all 768 image tokens.
All inputs are finite; a program needn't handle non-finite values.
Results may differ from the reference program's by a relative error of at most 0.0065.
Values may be sent and summed in bfloat16 or wider, within the bound.
No kernel may reach another device: no remote copies, remote signals or barrier semaphores. Data moves between devices by JAX's collectives and lax.ppermute only.
A program may use at most 64 MiB of HBM per device.

```python
import jax
import jax.numpy as jnp
from jax import lax

H = 64
KVH = 8
HD = 128
TILES = 4
TXT_DEV = 128
TXT = 12288
IMG = 768
IMG_TILE = 192
N_SECTION = 8


def float_pair(key):
    base = jax.random.fold_in(key, 11)
    key_query = jax.random.fold_in(base, 1)
    key_image = jax.random.fold_in(base, 2)
    image = jnp.clip(jax.random.normal(key_image, (N_SECTION, 2, IMG, KVH * HD), jnp.float32), -4.0, 4.0)
    query = jnp.clip(jax.random.normal(key_query, (N_SECTION, TXT, H * HD), jnp.float32), -4.0, 4.0)
    return (query, image)


def draw_queries(key, part):
    return float_pair(key)[0].astype(jnp.bfloat16)


def draw_image_kv(key, part):
    return float_pair(key)[1].astype(jnp.bfloat16)


def draw_visible(key, part):
    tiles_seen = jax.random.randint(jax.random.fold_in(key, 23), (TXT,), 0, TILES + 1)
    last_row = jnp.arange(TXT, dtype=jnp.int32) % TXT_DEV == TXT_DEV - 1
    tiles_seen = jnp.where(last_row, TILES, tiles_seen)
    return (tiles_seen * IMG_TILE).astype(jnp.int32)


def shard_levels(own_key, dims, cuts, low, top_value):
    level = 1.0
    for dim, shards_of in cuts:
        heights = jax.random.uniform(jax.random.fold_in(jax.random.fold_in(own_key, 6), dim), (shards_of,), jnp.float32, low / len(cuts), top_value / len(cuts))
        level = level * jnp.repeat(jnp.exp(heights), dims[dim] // shards_of).reshape((-1,) + (1,) * (len(dims) - 1 - dim))
    return level


def setup_inputs(seed: int = 0) -> dict:
    key_of = jax.random.split(jax.random.key(seed), 5)
    queries = draw_queries(jax.random.fold_in(key_of[4], 71), 0)
    image_kv = draw_image_kv(jax.random.fold_in(key_of[4], 71), 0)
    visible = draw_visible(jax.random.fold_in(key_of[4], 71), 0)
    gate = jnp.clip(0.3 + 1.7 * jax.random.uniform(key_of[3], (N_SECTION,), jnp.float32) ** shard_levels(key_of[3], (N_SECTION,), ((0, 8),), -0.2, 0.2), 0.3, 2.0)
    return dict(queries=queries, image_kv=image_kv, visible=visible, gate=gate)


def layer_attention(query_rows, keys, vals, seen, gate_value):
    rows = query_rows.shape[0]
    query = query_rows.astype(jnp.float32).reshape(rows, KVH, H // KVH, HD)
    scores = jnp.einsum('tkgd,nkd->kgtn', query, keys) / jnp.sqrt(jnp.float32(HD))
    positions = jnp.arange(IMG, dtype=jnp.int32)
    live = positions[None, :] < seen[:, None]
    capped = jnp.where(live, scores, -1e+30)
    top = lax.optimization_barrier(jnp.max(capped, axis=-1))
    expo = jnp.where(live, jnp.exp(capped - top[..., None]), 0.0)
    denom = lax.optimization_barrier(jnp.sum(expo, axis=-1))
    weights = expo.astype(jnp.bfloat16).astype(jnp.float32)
    acc = jnp.einsum('kgtn,nkd->kgtd', weights, vals)
    result = acc / jnp.where(denom > 0, denom, 1.0)[..., None]
    result = jnp.transpose(result, (2, 0, 1, 3)).reshape(rows, H * HD)
    result = jnp.where((seen > 0)[:, None], result, 0.0) * jnp.tanh(gate_value)
    return result.astype(jnp.bfloat16)

def reference(queries, image_kv, visible, gate):
    outputs = []
    blocks = TXT // TXT_DEV
    for layer in range(N_SECTION):
        keys = image_kv[layer, 0].astype(jnp.float32).reshape(IMG, KVH, HD)
        vals = image_kv[layer, 1].astype(jnp.float32).reshape(IMG, KVH, HD)
        query_blocks = queries[layer].reshape(blocks, TXT_DEV, H * HD)
        seen_blocks = visible.reshape(blocks, TXT_DEV)

        def run(pair):
            return layer_attention(pair[0], keys, vals, pair[1], gate[layer])
        outputs.append(lax.map(run, (query_blocks, seen_blocks)).reshape(TXT, H * HD))
    return jnp.stack(outputs, axis=0)
```

```python
import functools
import math

import jax
import jax.numpy as jnp
from jax import lax
from jax.experimental import pallas as pl
from jax.experimental.pallas import tpu as pltpu
from jax.sharding import Mesh, PartitionSpec as P

H = 64
KVH = 8
HD = 128
G = H // KVH
TILE = 192
NEG = -1e30

FINE = (("ylo", 4), ("core", 2), ("yhi", 2), ("x", 4), ("z", 12))
YRING = ("ylo", "core", "yhi")
LANES = 256
VMEM_BYTES = 16 << 20


def attend_kernel(first, last, gate_ref, q_ref, seen_ref, a_ref, b_ref, *refs):
    refs = list(refs)
    if first:
        old = None
    else:
        old, refs = refs[:3], refs[3:]
    factor = math.log2(math.e) / math.sqrt(HD)
    half = a_ref.shape[0] * a_ref.shape[2]
    count = a_ref.shape[2]
    keys = jnp.concatenate([a_ref[:, 0].reshape(half, HD), b_ref[:, 0].reshape(half, HD)], axis=0)
    vals = jnp.concatenate([a_ref[:, 1].reshape(half, HD), b_ref[:, 1].reshape(half, HD)], axis=0)
    total = 2 * half
    rows = q_ref.shape[1]
    heads = LANES // rows
    tile = lax.broadcasted_iota(jnp.int32, (count, LANES), 0) // (count // 4)
    for c in range(G * rows // LANES):
        lanes = slice(c * LANES, (c + 1) * LANES)
        query = jnp.concatenate(
            [q_ref[0, :, (c * heads + g) * HD : (c * heads + g + 1) * HD] for g in range(heads)], axis=0
        )
        seen = seen_ref[:, lanes]
        score = lax.dot_general(keys, query, (((1,), (1,)), ((), ())), preferred_element_type=jnp.float32)
        live = tile * TILE < seen
        score = jnp.where(live[None], score.reshape(total // count, count, LANES), NEG)
        top = jnp.max(jnp.max(score, axis=0), axis=0, keepdims=True)
        if first:
            new = top
        else:
            new = jnp.maximum(top, old[0][0, :, lanes])
        expo = jnp.exp2((score - new) * factor)
        denom = jnp.sum(jnp.sum(expo, axis=0), axis=0, keepdims=True)
        weights = expo.astype(jnp.bfloat16).reshape(total, LANES)
        acc = lax.dot_general(vals, weights, (((0,), (0,)), ((), ())), preferred_element_type=jnp.float32)
        if not first:
            scale = jnp.exp2((old[0][0, :, lanes] - new) * factor)
            denom = denom + old[1][0, :, lanes] * scale
            acc = acc + old[2][0, :, lanes] * scale
        if last:
            out_ref = refs[0]
            ratio = jnp.where(seen > 0, jnp.tanh(gate_ref[0]) / denom, 0.0)
            result = acc * ratio
            for g in range(heads):
                piece = result[:, g * rows : (g + 1) * rows].T
                out_ref[0, :, (c * heads + g) * HD : (c * heads + g + 1) * HD] = piece.astype(jnp.bfloat16)
        else:
            refs[0][0, :, lanes] = new
            refs[1][0, :, lanes] = denom
            refs[2][0, :, lanes] = acc


def attend(gate, queries, seen, halves, state, last):
    rows = queries.shape[1]
    lanes = G * rows
    steps, _, count, _ = halves[0].shape
    first = state is None
    stat_spec = pl.BlockSpec((1, 1, lanes), lambda k: (k, 0, 0))
    acc_spec = pl.BlockSpec((1, HD, lanes), lambda k: (k, 0, 0))
    state_specs = [stat_spec, stat_spec, acc_spec]
    query_spec = pl.BlockSpec((1, rows, G * HD), lambda k: (0, 0, k))
    half_spec = pl.BlockSpec((steps, 2, count, HD), lambda k: (0, 0, 0, k))
    in_specs = [
        pl.BlockSpec(memory_space=pltpu.SMEM),
        query_spec,
        pl.BlockSpec((1, lanes), lambda k: (0, 0)),
        half_spec,
        half_spec,
    ]
    operands = [gate, queries, seen, *halves]
    aliases = {}
    if not first:
        if not last:
            aliases = {len(operands) + i: i for i in range(3)}
        in_specs += state_specs
        operands += list(state)
    if last:
        out_shape = jax.ShapeDtypeStruct(queries.shape, jnp.bfloat16)
        out_specs = query_spec
    else:
        stat = jax.ShapeDtypeStruct((KVH, 1, lanes), jnp.float32)
        out_shape = [stat, stat, jax.ShapeDtypeStruct((KVH, HD, lanes), jnp.float32)]
        out_specs = state_specs
    total = 2 * steps * count
    return pl.pallas_call(
        functools.partial(attend_kernel, first, last),
        grid=(KVH,),
        in_specs=in_specs,
        out_specs=out_specs,
        out_shape=out_shape,
        input_output_aliases=aliases,
        name="attend",
        compiler_params=pltpu.CompilerParams(vmem_limit_bytes=VMEM_BYTES),
        cost_estimate=pl.CostEstimate(
            flops=4 * H * rows * total * HD,
            bytes_accessed=2 * H * rows * HD + 8 * H * rows * HD,
            transcendentals=H * rows * total,
        ),
    )(*operands)


def body(queries, image_kv, visible, gate):
    layers = image_kv.shape[0]
    ring = lax.axis_size("x")
    seen = jnp.tile(visible, G)[None]
    sent = jnp.repeat(image_kv[:, :, 0], lax.axis_size("yhi"), axis=0)
    mine = lax.all_to_all(sent, YRING, split_axis=0, concat_axis=0, tiled=True)
    mine = jnp.transpose(mine, (1, 0, 2))
    own = lax.all_gather(mine, "z")
    middle = own.shape[0] // 2
    low, high = own[:middle], own[middle:]
    up = [(i, (i + 1) % ring) for i in range(ring)]
    down = [(i, (i - 1) % ring) for i in range(ring)]
    low_left = lax.ppermute(low, "x", up)
    high_right = lax.ppermute(high, "x", down)
    high_left = lax.ppermute(high, "x", up)
    low_right = lax.ppermute(low, "x", down)
    low_far = lax.ppermute(low_left, "x", up)
    high_far = lax.ppermute(high_right, "x", down)
    state = attend(gate, queries, seen, (low, high), None, False)
    state = attend(gate, queries, seen, (low_left, high_right), state, False)
    state = attend(gate, queries, seen, (high_left, low_right), state, False)
    return attend(gate, queries, seen, (low_far, high_far), state, True)


def solution(mesh):
    fine = Mesh(mesh.devices.reshape([n for _, n in FINE]), [a for a, _ in FINE])
    section, dp = ("ylo", "core"), ("yhi", "x", "z")
    in_specs = (
        P(section, dp, None),
        P(None, None, section + dp, None),
        P(dp),
        P(section),
    )
    return jax.shard_map(body, mesh=fine, in_specs=in_specs, out_specs=P(section, dp, None), check_vma=False)
```

```python
import functools
import math

import jax
import jax.numpy as jnp
from jax import lax
from jax.experimental import pallas as pl
from jax.experimental.pallas import tpu as pltpu
from jax.sharding import Mesh, PartitionSpec as P

H = 64
KVH = 8
HD = 128
G = H // KVH
TILE = 192
NEG = -1e30

FINE = (("ylo", 4), ("core", 2), ("yhi", 2), ("x", 4), ("z", 12))
YRING = ("ylo", "core", "yhi")
LANES = 512
ONES = 16
VMEM_BYTES = 24 << 20


def attend_kernel(first, last, gate_ref, q_ref, seen_ref, bias_ref, a_ref, b_ref, *refs):
    old, refs = (None, refs) if first else (refs[:3], refs[3:])
    *refs, score_ref, weight_ref = refs
    factor = math.log2(math.e) / math.sqrt(HD)
    half = a_ref.shape[0] * a_ref.shape[2]
    count = a_ref.shape[2]
    total = 2 * half
    rows = q_ref.shape[1]
    heads = LANES // rows
    row = lax.broadcasted_iota(jnp.int32, (total, HD), 0)
    lane = lax.broadcasted_iota(jnp.int32, (total, HD), 1)
    chosen = (lane == row % count // (count // 4)).astype(jnp.bfloat16)
    ones = jnp.ones((ONES, total), jnp.bfloat16)

    def store(k):
        out_ref, made, sems = refs
        columns = pl.ds(pl.multiple_of(k * G * HD, G * HD), G * HD)
        return pltpu.make_async_copy(made.at[:, columns], out_ref.at[0, :, columns], sems.at[k])

    def columns_of(k):
        return pl.ds(pl.multiple_of(k * HD, HD), HD)

    def wide(k, c, g):
        return pl.ds(pl.multiple_of(k * G * HD + (c * heads + g) * HD, HD), HD)

    def both(k, which):
        columns = columns_of(k)
        return jnp.concatenate(
            [a_ref[:, which, :, columns].reshape(half, HD), b_ref[:, which, :, columns].reshape(half, HD)], axis=0
        )

    def scores(k, c):
        query = jnp.concatenate(
            [jnp.concatenate([q_ref[0, :, wide(k, c, g)], bias_ref[...]], axis=1) for g in range(heads)], axis=0
        )
        keys = jnp.concatenate([both(k, 0), chosen], axis=1)
        score = lax.dot_general(keys, query, (((1,), (1,)), ((), ())), preferred_element_type=jnp.float32)
        score = score.reshape(total // 8, 8, LANES)
        score_ref[c % 2] = score
        return jnp.max(score, axis=0)

    def finish(k, c, top, vals):
        lanes = slice(c * LANES, (c + 1) * LANES)
        top = jnp.max(top, axis=0, keepdims=True)
        new = top if first else jnp.maximum(top, old[0][k, :, lanes])
        expo = jnp.exp2((score_ref[c % 2] - new) * factor)
        weight_ref[c % 2] = expo.astype(jnp.bfloat16).reshape(total, LANES)
        summed = jnp.dot(vals, weight_ref[c % 2], preferred_element_type=jnp.float32)
        acc, denom = summed[:HD], summed[HD : HD + 1]
        if not first:
            scale = jnp.exp2((old[0][k, :, lanes] - new) * factor)
            denom = denom + old[1][k, :, lanes] * scale
            acc = acc + old[2][k, :, lanes] * scale
        if last:
            ratio = jnp.where(seen_ref[:, lanes] > 0, jnp.tanh(gate_ref[0]) / denom, 0.0)
            result = acc * ratio
            for g in range(heads):
                piece = result[:, g * rows : (g + 1) * rows].T
                refs[1][:, wide(k, c, g)] = piece.astype(jnp.bfloat16)
        else:
            refs[0][k, :, lanes] = new
            refs[1][k, :, lanes] = denom
            refs[2][k, :, lanes] = acc

    chunks = G * rows // LANES

    def head(k, top):
        vals = jnp.concatenate([both(k, 1).T, ones], axis=0)
        for c in range(chunks):
            ahead = scores(k, c + 1) if c + 1 < chunks else scores(jnp.minimum(k + 1, KVH - 1), 0)
            finish(k, c, top, vals)
            top = ahead
        if last:
            store(k).start()
        return top

    lax.fori_loop(0, KVH, head, scores(0, 0), unroll=2)
    if last:
        lax.fori_loop(0, KVH, lambda k, carry: (store(k).wait(), carry)[1], 0)


def attend(gate, queries, seen, bias, halves, state, last):
    rows = queries.shape[1]
    lanes = G * rows
    steps, _, count, _ = halves[0].shape
    first = state is None
    vmem = pl.BlockSpec(memory_space=pltpu.VMEM)
    operands = [gate, queries, seen, bias, *halves]
    in_specs = [pl.BlockSpec(memory_space=pltpu.SMEM)] + [vmem] * 5
    aliases = {}
    total = 2 * steps * count
    buffers = [
        pltpu.VMEM((2, total // 8, 8, LANES), jnp.float32),
        pltpu.VMEM((2, total, LANES), jnp.bfloat16),
    ]
    scratch = []
    if not first:
        if not last:
            aliases = {len(operands) + i: i for i in range(3)}
        in_specs += [vmem] * 3
        operands += list(state)
    if last:
        out_shape = jax.ShapeDtypeStruct(queries.shape, jnp.bfloat16)
        out_specs = pl.BlockSpec(memory_space=pl.ANY)
        scratch = [pltpu.VMEM((rows, H * HD), jnp.bfloat16), pltpu.SemaphoreType.DMA((KVH,))]
    else:
        stat = jax.ShapeDtypeStruct((KVH, 1, lanes), jnp.float32)
        out_shape = [stat, stat, jax.ShapeDtypeStruct((KVH, HD, lanes), jnp.float32)]
        out_specs = [vmem] * 3
    return pl.pallas_call(
        functools.partial(attend_kernel, first, last),
        in_specs=in_specs,
        out_specs=out_specs,
        out_shape=out_shape,
        scratch_shapes=scratch + buffers,
        input_output_aliases=aliases,
        name="attend",
        compiler_params=pltpu.CompilerParams(vmem_limit_bytes=VMEM_BYTES),
        cost_estimate=pl.CostEstimate(
            flops=4 * H * rows * total * HD,
            bytes_accessed=2 * H * rows * HD + 8 * H * rows * HD,
            transcendentals=H * rows * total,
        ),
    )(*operands)


def body(queries, image_kv, visible, gate):
    layers = image_kv.shape[0]
    ring = lax.axis_size("x")
    seen = jnp.tile(visible, G)[None]
    starts = jnp.arange(HD, dtype=jnp.int32) * TILE
    bias = jnp.where(starts < visible[:, None], 0.0, NEG).astype(jnp.bfloat16)
    sent = jnp.repeat(image_kv[:, :, 0], lax.axis_size("yhi"), axis=0)
    mine = lax.all_to_all(sent, YRING, split_axis=0, concat_axis=0, tiled=True)
    mine = jnp.transpose(mine, (1, 0, 2))
    own = lax.all_gather(mine, "z")
    middle = own.shape[0] // 2
    low, high = own[:middle], own[middle:]
    up = [(i, (i + 1) % ring) for i in range(ring)]
    down = [(i, (i - 1) % ring) for i in range(ring)]
    low_left = lax.ppermute(low, "x", up)
    high_right = lax.ppermute(high, "x", down)
    high_left = lax.ppermute(high, "x", up)
    low_right = lax.ppermute(low, "x", down)
    low_far = lax.ppermute(low_left, "x", up)
    high_far = lax.ppermute(high_right, "x", down)
    state = attend(gate, queries, seen, bias, (low, high), None, False)
    state = attend(gate, queries, seen, bias, (low_left, high_right), state, False)
    state = attend(gate, queries, seen, bias, (high_left, low_right), state, False)
    return attend(gate, queries, seen, bias, (low_far, high_far), state, True)


def solution(mesh):
    fine = Mesh(mesh.devices.reshape([n for _, n in FINE]), [a for a, _ in FINE])
    section, dp = ("ylo", "core"), ("yhi", "x", "z")
    in_specs = (
        P(section, dp, None),
        P(None, None, section + dp, None),
        P(dp),
        P(section),
    )
    return jax.shard_map(body, mesh=fine, in_specs=in_specs, out_specs=P(section, dp, None), check_vma=False)
```

```python
import functools
import math

import jax
import jax.numpy as jnp
from jax import lax
from jax.experimental import pallas as pl
from jax.experimental.pallas import tpu as pltpu
from jax.sharding import Mesh, PartitionSpec as P

H = 64
KVH = 8
HD = 128
G = H // KVH
TILE = 192
NEG = -1e30

FINE = (("ylo", 4), ("core", 2), ("yhi", 2), ("x", 4), ("z", 12))
YRING = ("ylo", "core", "yhi")
LANES = 512
ONES = 16
VMEM_BYTES = 24 << 20


def attend_kernel(first, last, parts, gate_ref, q_ref, seen_ref, *refs):
    part_refs, refs = refs[:parts], refs[parts:]
    old, refs = (None, refs) if first else (refs[:3], refs[3:])
    *refs, score_ref, weight_ref = refs
    factor = math.log2(math.e) / math.sqrt(HD)
    count = part_refs[0].shape[2]
    sizes = [p.shape[0] * count for p in part_refs]
    total = sum(sizes)
    rows = q_ref.shape[1]
    heads = LANES // rows
    reach = jnp.broadcast_to(seen_ref[...].astype(jnp.float32), (HD, rows)).T
    starts = (lax.broadcasted_iota(jnp.int32, (rows, HD), 1) * TILE).astype(jnp.float32)
    bias = jnp.where(starts < reach, 0.0, NEG).astype(jnp.bfloat16)
    row = lax.broadcasted_iota(jnp.int32, (total, HD), 0)
    lane = lax.broadcasted_iota(jnp.int32, (total, HD), 1)
    chosen = (lane == row % count // (count // 4)).astype(jnp.bfloat16)
    ones = jnp.ones((ONES, total), jnp.bfloat16)
    seen = jnp.concatenate([seen_ref[...]] * heads, axis=1)

    def store(k):
        out_ref, made, sems = refs
        columns = pl.ds(pl.multiple_of(k * G * HD, G * HD), G * HD)
        return pltpu.make_async_copy(made.at[:, columns], out_ref.at[0, :, columns], sems.at[k])

    def wide(k, c, g):
        return pl.ds(pl.multiple_of(k * G * HD + (c * heads + g) * HD, HD), HD)

    def gather(k, which):
        columns = pl.ds(pl.multiple_of(k * HD, HD), HD)
        return jnp.concatenate(
            [p[:, which, :, columns].reshape(n, HD) for p, n in zip(part_refs, sizes)], axis=0
        )

    def scores(k, c):
        query = jnp.concatenate(
            [jnp.concatenate([q_ref[0, :, wide(k, c, g)], bias], axis=1) for g in range(heads)], axis=0
        )
        keys = jnp.concatenate([gather(k, 0), chosen], axis=1)
        score = lax.dot_general(keys, query, (((1,), (1,)), ((), ())), preferred_element_type=jnp.float32)
        score = score.reshape(total // 8, 8, LANES)
        score_ref[c % 2] = score
        return jnp.max(score, axis=0)

    def finish(k, c, top, vals):
        lanes = slice(c * LANES, (c + 1) * LANES)
        top = jnp.max(top, axis=0, keepdims=True)
        new = top if first else jnp.maximum(top, old[0][k, :, lanes])
        expo = jnp.exp2((score_ref[c % 2] - new) * factor)
        weight_ref[c % 2] = expo.astype(jnp.bfloat16).reshape(total, LANES)
        summed = jnp.dot(vals, weight_ref[c % 2], preferred_element_type=jnp.float32)
        acc, denom = summed[:HD], summed[HD : HD + 1]
        if not first:
            scale = jnp.exp2((old[0][k, :, lanes] - new) * factor)
            denom = denom + old[1][k, :, lanes] * scale
            acc = acc + old[2][k, :, lanes] * scale
        if last:
            ratio = jnp.where(seen > 0, jnp.tanh(gate_ref[0]) / denom, 0.0)
            result = (acc * ratio).astype(jnp.bfloat16)
            for g in range(heads):
                refs[1][:, wide(k, c, g)] = result[:, g * rows : (g + 1) * rows].T
        else:
            refs[0][k, :, lanes] = new
            refs[1][k, :, lanes] = denom
            refs[2][k, :, lanes] = acc

    chunks = G * rows // LANES

    def head(k, top):
        vals = jnp.concatenate([gather(k, 1).T, ones], axis=0)
        for c in range(chunks):
            if c + 1 < chunks:
                ahead = scores(k, c + 1)
            else:
                ahead = scores(jnp.minimum(k + 1, KVH - 1), 0)
            finish(k, c, top, vals)
            top = ahead
        if last:
            store(k).start()
        return top

    lax.fori_loop(0, KVH, head, scores(0, 0), unroll=4)
    if last:
        lax.fori_loop(0, KVH, lambda k, carry: (store(k).wait(), carry)[1], 0)


def attend(gate, queries, seen, parts, state, last):
    rows = queries.shape[1]
    lanes = G * rows
    count = parts[0].shape[2]
    first = state is None
    vmem = pl.BlockSpec(memory_space=pltpu.VMEM)
    operands = [gate, queries, seen, *parts]
    in_specs = [pl.BlockSpec(memory_space=pltpu.SMEM)] + [vmem] * (2 + len(parts))
    aliases = {}
    total = sum(p.shape[0] * count for p in parts)
    buffers = [
        pltpu.VMEM((2, total // 8, 8, LANES), jnp.float32),
        pltpu.VMEM((2, total, LANES), jnp.bfloat16),
    ]
    scratch = []
    if not first:
        if not last:
            aliases = {len(operands) + i: i for i in range(3)}
        in_specs += [vmem] * 3
        operands += list(state)
    if last:
        out_shape = jax.ShapeDtypeStruct(queries.shape, jnp.bfloat16)
        out_specs = pl.BlockSpec(memory_space=pl.ANY)
        scratch = [pltpu.VMEM((rows, H * HD), jnp.bfloat16), pltpu.SemaphoreType.DMA((KVH,))]
    else:
        stat = jax.ShapeDtypeStruct((KVH, 1, lanes), jnp.float32)
        out_shape = [stat, stat, jax.ShapeDtypeStruct((KVH, HD, lanes), jnp.float32)]
        out_specs = [vmem] * len(out_shape)
    return pl.pallas_call(
        functools.partial(attend_kernel, first, last, len(parts)),
        in_specs=in_specs,
        out_specs=out_specs,
        out_shape=out_shape,
        scratch_shapes=scratch + buffers,
        input_output_aliases=aliases,
        name="attend",
        compiler_params=pltpu.CompilerParams(vmem_limit_bytes=VMEM_BYTES),
        cost_estimate=pl.CostEstimate(
            flops=4 * H * rows * total * HD,
            bytes_accessed=2 * H * rows * HD + 8 * H * rows * HD,
            transcendentals=H * rows * total,
        ),
    )(*operands)


def body(queries, image_kv, visible, gate):
    ring = lax.axis_size("x")
    seen = visible[None]
    sent = jnp.repeat(image_kv[:, :, 0], lax.axis_size("yhi"), axis=0)
    mine = lax.all_to_all(sent, YRING, split_axis=0, concat_axis=0, tiled=True)
    mine = jnp.transpose(mine, (1, 0, 2))
    own = lax.all_gather(mine, "z")
    middle = own.shape[0] // 2
    low, high = own[:middle], own[middle:]
    up = [(i, (i + 1) % ring) for i in range(ring)]
    down = [(i, (i - 1) % ring) for i in range(ring)]
    low_left = lax.ppermute(low, "x", up)
    high_right = lax.ppermute(high, "x", down)
    high_left = lax.ppermute(high, "x", up)
    low_right = lax.ppermute(low, "x", down)
    low_far = lax.ppermute(low_left, "x", up)
    high_far = lax.ppermute(high_right, "x", down)
    state = attend(gate, queries, seen, (low, high, low_left, high_right), None, False)
    return attend(gate, queries, seen, (high_left, low_right, low_far, high_far), state, True)


def solution(mesh):
    fine = Mesh(mesh.devices.reshape([n for _, n in FINE]), [a for a, _ in FINE])
    section, dp = ("ylo", "core"), ("yhi", "x", "z")
    in_specs = (
        P(section, dp, None),
        P(None, None, section + dp, None),
        P(dp),
        P(section),
    )
    return jax.shard_map(body, mesh=fine, in_specs=in_specs, out_specs=P(section, dp, None), check_vma=False)
```

```python
import functools
import math

import jax
import jax.numpy as jnp
from jax import lax
from jax.experimental import pallas as pl
from jax.experimental.pallas import tpu as pltpu
from jax.sharding import Mesh, PartitionSpec as P

H = 64
KVH = 8
HD = 128
G = H // KVH
TILE = 192
NEG = -1e30

FINE = (("ylo", 4), ("core", 2), ("yhi", 2), ("x", 4), ("z", 12))
YRING = ("ylo", "core", "yhi")
LANES = 512
ONES = 16
VMEM_BYTES = 24 << 20


def attend_kernel(first, last, parts, gate_ref, q_ref, seen_ref, *refs):
    part_refs, refs = refs[:parts], refs[parts:]
    old, refs = (None, refs) if first else (refs[:3], refs[3:])
    *refs, score_ref, weight_ref = refs
    factor = math.log2(math.e) / math.sqrt(HD)
    count = part_refs[0].shape[2]
    sizes = [p.shape[0] * count for p in part_refs]
    total = sum(sizes)
    rows = q_ref.shape[1]
    heads = LANES // rows
    reach = jnp.broadcast_to(seen_ref[...].astype(jnp.float32), (HD, rows)).T
    starts = (lax.broadcasted_iota(jnp.int32, (rows, HD), 1) * TILE).astype(jnp.float32)
    bias = jnp.where(starts < reach, 0.0, NEG).astype(jnp.bfloat16)
    row = lax.broadcasted_iota(jnp.int32, (total, HD), 0)
    lane = lax.broadcasted_iota(jnp.int32, (total, HD), 1)
    chosen = (lane == row % count // (count // 4)).astype(jnp.bfloat16)
    ones = jnp.ones((ONES, total), jnp.bfloat16)
    seen = jnp.concatenate([seen_ref[...]] * heads, axis=1)

    def store(k):
        out_ref, made, sems = refs
        columns = pl.ds(pl.multiple_of(k * G * HD, G * HD), G * HD)
        return pltpu.make_async_copy(made.at[:, columns], out_ref.at[0, :, columns], sems.at[k])

    def wide(k, c, g):
        return pl.ds(pl.multiple_of(k * G * HD + (c * heads + g) * HD, HD), HD)

    def gather(k, which):
        columns = pl.ds(pl.multiple_of(k * HD, HD), HD)
        return jnp.concatenate(
            [p[:, which, :, columns].reshape(n, HD) for p, n in zip(part_refs, sizes)], axis=0
        )

    def scores(k, c):
        query = jnp.concatenate(
            [jnp.concatenate([q_ref[0, :, wide(k, c, g)], bias], axis=1) for g in range(heads)], axis=0
        )
        keys = jnp.concatenate([gather(k, 0), chosen], axis=1)
        score = lax.dot_general(keys, query, (((1,), (1,)), ((), ())), preferred_element_type=jnp.float32)
        score = score.reshape(total // 8, 8, LANES)
        score_ref[c % 2] = score
        return jnp.max(score, axis=0)

    def finish(k, c, top, vals):
        lanes = slice(c * LANES, (c + 1) * LANES)
        top = jnp.max(top, axis=0, keepdims=True)
        new = top if first else jnp.maximum(top, old[0][k, :, lanes])
        expo = jnp.exp2((score_ref[c % 2] - new) * factor)
        weight_ref[c % 2] = expo.astype(jnp.bfloat16).reshape(total, LANES)
        summed = jnp.dot(vals, weight_ref[c % 2], preferred_element_type=jnp.float32)
        acc, denom = summed[:HD], summed[HD : HD + 1]
        if not first:
            scale = jnp.exp2((old[0][k, :, lanes] - new) * factor)
            denom = denom + old[1][k, :, lanes] * scale
            acc = acc + old[2][k, :, lanes] * scale
        if last:
            ratio = jnp.where(seen > 0, jnp.tanh(gate_ref[0]) / denom, 0.0)
            result = (acc * ratio).astype(jnp.bfloat16)
            for g in range(heads):
                refs[1][:, wide(k, c, g)] = result[:, g * rows : (g + 1) * rows].T
        else:
            refs[0][k, :, lanes] = new
            refs[1][k, :, lanes] = denom
            refs[2][k, :, lanes] = acc

    chunks = G * rows // LANES

    def head(k, top):
        vals = jnp.concatenate([gather(k, 1).T, ones], axis=0)
        for c in range(chunks):
            if c + 1 < chunks:
                ahead = scores(k, c + 1)
            else:
                ahead = scores(jnp.minimum(k + 1, KVH - 1), 0)
            finish(k, c, top, vals)
            top = ahead
        if last:
            store(k).start()
        return top

    lax.fori_loop(0, KVH, head, scores(0, 0), unroll=8 if last else 4)
    if last:
        lax.fori_loop(0, KVH, lambda k, carry: (store(k).wait(), carry)[1], 0)


def attend(gate, queries, seen, parts, state, last):
    rows = queries.shape[1]
    lanes = G * rows
    count = parts[0].shape[2]
    first = state is None
    vmem = pl.BlockSpec(memory_space=pltpu.VMEM)
    operands = [gate, queries, seen, *parts]
    in_specs = [pl.BlockSpec(memory_space=pltpu.SMEM)] + [vmem] * (2 + len(parts))
    aliases = {}
    total = sum(p.shape[0] * count for p in parts)
    buffers = [
        pltpu.VMEM((2, total // 8, 8, LANES), jnp.float32),
        pltpu.VMEM((2, total, LANES), jnp.bfloat16),
    ]
    scratch = []
    if not first:
        if not last:
            aliases = {len(operands) + i: i for i in range(3)}
        in_specs += [vmem] * 3
        operands += list(state)
    if last:
        out_shape = jax.ShapeDtypeStruct(queries.shape, jnp.bfloat16)
        out_specs = pl.BlockSpec(memory_space=pl.ANY)
        scratch = [pltpu.VMEM((rows, H * HD), jnp.bfloat16), pltpu.SemaphoreType.DMA((KVH,))]
    else:
        stat = jax.ShapeDtypeStruct((KVH, 1, lanes), jnp.float32)
        out_shape = [stat, stat, jax.ShapeDtypeStruct((KVH, HD, lanes), jnp.float32)]
        out_specs = [vmem] * len(out_shape)
    return pl.pallas_call(
        functools.partial(attend_kernel, first, last, len(parts)),
        in_specs=in_specs,
        out_specs=out_specs,
        out_shape=out_shape,
        scratch_shapes=scratch + buffers,
        input_output_aliases=aliases,
        name="attend",
        compiler_params=pltpu.CompilerParams(vmem_limit_bytes=VMEM_BYTES),
    )(*operands)


def body(queries, image_kv, visible, gate):
    ring = lax.axis_size("x")
    seen = visible[None]
    sent = jnp.repeat(image_kv[:, :, 0], lax.axis_size("yhi"), axis=0)
    mine = lax.all_to_all(sent, YRING, split_axis=0, concat_axis=0, tiled=True)
    mine = jnp.transpose(mine, (1, 0, 2))
    own = lax.all_gather(mine, "z")
    middle = own.shape[0] // 2
    low, high = own[:middle], own[middle:]
    up = [(i, (i + 1) % ring) for i in range(ring)]
    down = [(i, (i - 1) % ring) for i in range(ring)]
    low_left = lax.ppermute(low, "x", up)
    high_right = lax.ppermute(high, "x", down)
    high_left = lax.ppermute(high, "x", up)
    low_right = lax.ppermute(low, "x", down)
    low_far = lax.ppermute(low_left, "x", up)
    high_far = lax.ppermute(high_right, "x", down)
    state = attend(gate, queries, seen, (low, high, low_left, high_right), None, False)
    state = attend(gate, queries, seen, (high_left, low_right), state, False)
    return attend(gate, queries, seen, (low_far, high_far), state, True)


def solution(mesh):
    fine = Mesh(mesh.devices.reshape([n for _, n in FINE]), [a for a, _ in FINE])
    section, dp = ("ylo", "core"), ("yhi", "x", "z")
    in_specs = (
        P(section, dp, None),
        P(None, None, section + dp, None),
        P(dp),
        P(section),
    )
    return jax.shard_map(body, mesh=fine, in_specs=in_specs, out_specs=P(section, dp, None), check_vma=False)
```

```python
import functools
import math

import jax
import jax.numpy as jnp
from jax import lax
from jax.experimental import pallas as pl
from jax.experimental.pallas import tpu as pltpu
from jax.sharding import Mesh, PartitionSpec as P

H = 64
KVH = 8
HD = 128
G = H // KVH
TILE = 192
NEG = -1e30

FINE = (("ylo", 4), ("core", 2), ("yhi", 2), ("x", 4), ("z", 12))
YRING = ("ylo", "core", "yhi")
LANES = 512
ONES = 16
VMEM_BYTES = 24 << 20


def attend_kernel(first, last, parts, gate_ref, q_ref, seen_ref, *refs):
    part_refs, refs = refs[:parts], refs[parts:]
    old, refs = (None, refs) if first else (refs[:3], refs[3:])
    *refs, score_ref, weight_ref = refs
    factor = math.log2(math.e) / math.sqrt(HD)
    count = part_refs[0].shape[2]
    sizes = [p.shape[0] * count for p in part_refs]
    total = sum(sizes)
    rows = q_ref.shape[1]
    heads = LANES // rows
    reach = jnp.broadcast_to(seen_ref[...].astype(jnp.float32), (HD, rows)).T
    starts = (lax.broadcasted_iota(jnp.int32, (rows, HD), 1) * TILE).astype(jnp.float32)
    bias = jnp.where(starts < reach, 0.0, NEG).astype(jnp.bfloat16)
    row = lax.broadcasted_iota(jnp.int32, (total, HD), 0)
    lane = lax.broadcasted_iota(jnp.int32, (total, HD), 1)
    chosen = (lane == row % count // (count // 4)).astype(jnp.bfloat16)
    ones = jnp.ones((ONES, total), jnp.bfloat16)
    seen = jnp.concatenate([seen_ref[...]] * heads, axis=1)

    def store(k):
        out_ref, made, sems = refs
        columns = pl.ds(pl.multiple_of(k * G * HD, G * HD), G * HD)
        return pltpu.make_async_copy(made.at[:, columns], out_ref.at[0, :, columns], sems.at[k])

    def wide(k, c, g):
        return pl.ds(pl.multiple_of(k * G * HD + (c * heads + g) * HD, HD), HD)

    def gather(k, which):
        columns = pl.ds(pl.multiple_of(k * HD, HD), HD)
        return jnp.concatenate(
            [p[:, which, :, columns].reshape(n, HD) for p, n in zip(part_refs, sizes)], axis=0
        )

    def scores(k, c):
        query = jnp.concatenate(
            [jnp.concatenate([q_ref[0, :, wide(k, c, g)], bias], axis=1) for g in range(heads)], axis=0
        )
        keys = jnp.concatenate([gather(k, 0), chosen], axis=1)
        score = lax.dot_general(keys, query, (((1,), (1,)), ((), ())), preferred_element_type=jnp.float32)
        score = score.reshape(total // 8, 8, LANES)
        score_ref[c % 2] = score
        return jnp.max(score, axis=0)

    def finish(k, c, top, vals):
        lanes = slice(c * LANES, (c + 1) * LANES)
        top = jnp.max(top, axis=0, keepdims=True)
        new = top if first else jnp.maximum(top, old[0][k, :, lanes])
        expo = jnp.exp2((score_ref[c % 2] - new) * factor)
        weight_ref[c % 2] = expo.astype(jnp.bfloat16).reshape(total, LANES)
        summed = jnp.dot(vals, weight_ref[c % 2], preferred_element_type=jnp.float32)
        acc, denom = summed[:HD], summed[HD : HD + 1]
        if not first:
            scale = jnp.exp2((old[0][k, :, lanes] - new) * factor)
            denom = denom + old[1][k, :, lanes] * scale
            acc = acc + old[2][k, :, lanes] * scale
        if last:
            ratio = jnp.where(seen > 0, jnp.tanh(gate_ref[0]) / denom, 0.0)
            result = (acc * ratio).astype(jnp.bfloat16)
            for g in range(heads):
                refs[1][:, wide(k, c, g)] = result[:, g * rows : (g + 1) * rows].T
        else:
            refs[0][k, :, lanes] = new
            refs[1][k, :, lanes] = denom
            refs[2][k, :, lanes] = acc

    chunks = G * rows // LANES

    def head(k, top):
        vals = jnp.concatenate([gather(k, 1).T, ones], axis=0)
        for c in range(chunks):
            if c + 1 < chunks:
                ahead = scores(k, c + 1)
            else:
                ahead = scores(jnp.minimum(k + 1, KVH - 1), 0)
            finish(k, c, top, vals)
            top = ahead
        if last:
            store(k).start()
        return top

    lax.fori_loop(0, KVH, head, scores(0, 0), unroll=8 if last else 4)
    if last:
        lax.fori_loop(0, KVH, lambda k, carry: (store(k).wait(), carry)[1], 0)


def attend(gate, queries, seen, parts, state, last):
    rows = queries.shape[1]
    lanes = G * rows
    count = parts[0].shape[2]
    first = state is None
    vmem = pl.BlockSpec(memory_space=pltpu.VMEM)
    operands = [gate, queries, seen, *parts]
    in_specs = [pl.BlockSpec(memory_space=pltpu.SMEM)] + [vmem] * (2 + len(parts))
    aliases = {}
    total = sum(p.shape[0] * count for p in parts)
    buffers = [
        pltpu.VMEM((2, total // 8, 8, LANES), jnp.float32),
        pltpu.VMEM((2, total, LANES), jnp.bfloat16),
    ]
    scratch = []
    if not first:
        if not last:
            aliases = {len(operands) + i: i for i in range(3)}
        in_specs += [vmem] * 3
        operands += list(state)
    if last:
        out_shape = jax.ShapeDtypeStruct(queries.shape, jnp.bfloat16)
        out_specs = pl.BlockSpec(memory_space=pl.ANY)
        scratch = [pltpu.VMEM((rows, H * HD), jnp.bfloat16), pltpu.SemaphoreType.DMA((KVH,))]
    else:
        stat = jax.ShapeDtypeStruct((KVH, 1, lanes), jnp.float32)
        out_shape = [stat, stat, jax.ShapeDtypeStruct((KVH, HD, lanes), jnp.float32)]
        out_specs = [vmem] * len(out_shape)
    return pl.pallas_call(
        functools.partial(attend_kernel, first, last, len(parts)),
        in_specs=in_specs,
        out_specs=out_specs,
        out_shape=out_shape,
        scratch_shapes=scratch + buffers,
        input_output_aliases=aliases,
        name="attend",
        compiler_params=pltpu.CompilerParams(vmem_limit_bytes=VMEM_BYTES),
    )(*operands)


def body(queries, image_kv, visible, gate):
    ring = lax.axis_size("x")
    seen = visible[None]
    sent = jnp.repeat(image_kv[:, :, 0], lax.axis_size("yhi"), axis=0)
    mine = lax.all_to_all(sent, YRING, split_axis=0, concat_axis=0, tiled=True)
    mine = jnp.transpose(mine, (1, 0, 2))
    own = lax.all_gather(mine, "z")
    middle = own.shape[0] // 2
    low, high = own[:middle], own[middle:]
    up = [(i, (i + 1) % ring) for i in range(ring)]
    down = [(i, (i - 1) % ring) for i in range(ring)]
    low_left = lax.ppermute(low, "x", up)
    high_right = lax.ppermute(high, "x", down)
    high_left = lax.ppermute(high, "x", up)
    low_right = lax.ppermute(low, "x", down)
    low_far = lax.ppermute(low_left, "x", up)
    high_far = lax.ppermute(high_right, "x", down)
    state = attend(gate, queries, seen, (low, high, low_left, high_right), None, False)
    state = attend(gate, queries, seen, (high_left, low_right, low_far), state, False)
    return attend(gate, queries, seen, (high_far,), state, True)


def solution(mesh):
    fine = Mesh(mesh.devices.reshape([n for _, n in FINE]), [a for a, _ in FINE])
    section, dp = ("ylo", "core"), ("yhi", "x", "z")
    in_specs = (
        P(section, dp, None),
        P(None, None, section + dp, None),
        P(dp),
        P(section),
    )
    return jax.shard_map(body, mesh=fine, in_specs=in_specs, out_specs=P(section, dp, None), check_vma=False)
```
